512 devices in a mesh: tensor: 16 (over x_lo, y), adapter: 32 (over x_hi, z, core).
Axes of the slice: x: 4 (x_hi: 2, x_lo: 2; x = x_hi * 2 + x_lo), y: 8, z: 8, core: 2. Of those that a mesh axis runs over, the one named last changes fastest.
Arguments:
- tokens: bfloat16 [65536, 8192], P(('tensor', 'adapter')), may hold values from -6 to 6
- base_key_weight: bfloat16 [8192, 768], P(None, 'tensor'), may hold values from -0.0625 to 0.0625
- adapter_down_factors: bfloat16 [32, 8192, 64], P('adapter'), may hold values from -0.0625 to 0.0625
- adapter_up_factors: bfloat16 [32, 64, 768], P('adapter'), may hold values from -0.75 to 0.75
- token_adapter_index: int32 [65536, 1], P(('tensor', 'adapter')), may hold values from 0 to 31; in each aligned block of 128 rows (0 to 127, 128 to 255, ...) at most 8 rows name the same one
- placement: int32 [32], replicated, may hold values from 0 to 31, each once
Outputs:
- keys_out: bfloat16 [65536, 768], P(('tensor', 'adapter'))
The draws below stay inside these ranges and needn't reach their ends.
Inputs may be any that keep to these rules, and one draw needn't show every extreme that they name: `token_adapter_index`: in each aligned block of 128 tokens (the tokens of one device) no adapter is named by more than 8 tokens, a bound that some block reaches. `placement`: each slot holds exactly one adapter.
All inputs are finite; a program needn't handle non-finite values.
Results may differ from the reference program's by a relative error of at most 0.005.
Values may be sent and summed in bfloat16 or wider, within the bound.
No kernel may reach another device: no remote copies, remote signals or barrier semaphores. Data moves between devices by JAX's collectives and lax.ppermute only.
A program may use at most 64 MiB of HBM per device.

```python
import math
import jax
import jax.numpy as jnp
import numpy as np
from jax import lax

MODEL_WIDTH = 8192
KEY_COLUMNS = 768
ADAPTER_RANK = 64
TOK_DEV = 128
ADAPTER_COUNT = 32
CAP = 8
TOKENS = 65536


def level_of(rng, dims, cuts, smallest, largest):
    factor_of = 1.0
    for axis_at, shards_of in cuts:
        draws = jax.random.uniform(jax.random.fold_in(jax.random.fold_in(rng, 6), axis_at), (shards_of,), jnp.float32, smallest / len(cuts), largest / len(cuts))
        factor_of = factor_of * jnp.repeat(jnp.exp(draws), dims[axis_at] // shards_of).reshape((-1,) + (1,) * (len(dims) - 1 - axis_at))
    return factor_of


def routed_block(key, own, number, rows, number_of, top, most, lean):
    sequence = jax.random.permutation(key, number_of)
    crowded, ordinary = portions_of(number_of, rows * top, most, lean, True), portions_of(number_of, rows * top, most, lean, False)
    places = jnp.arange(number_of)

    def named(sizes, turn):
        used = int((sizes > 0).sum())
        fixed = max(1, used // 4)
        shifted = fixed + (places - fixed + turn * (used - fixed)) % max(1, number_of - fixed)
        return jnp.zeros((number_of,), jnp.int32).at[sequence[jnp.where(places < fixed, places, shifted)]].set(jnp.asarray(sizes, jnp.int32))

    sizes = jnp.where(number % 4 == 0, named(crowded, number // 4), named(ordinary, number - number // 4 - 1))
    mixed = jax.random.permutation(jax.random.fold_in(own, 3), number_of)
    source_of, taker = mixed[0:number_of // 2 * 2:2], mixed[1:number_of // 2 * 2:2]
    room = jnp.minimum(sizes[source_of] - 1, most - sizes[taker]) // 2
    room = jnp.where((source_of == sequence[0]) | (taker == sequence[0]) | (sizes[taker] == 0), 0, jnp.maximum(room, 0))
    shifted = jax.random.randint(jax.random.fold_in(own, 4), (number_of // 2,), 0, 1 << 20) % (room + 1)
    sizes = sizes.at[source_of].add(-shifted).at[taker].add(shifted)
    labels = jnp.searchsorted(jnp.cumsum(sizes), jnp.arange(rows * top), side="right").astype(jnp.int32)
    listing = labels.reshape(top, rows).T
    listing = listing[jax.random.permutation(jax.random.fold_in(own, 1), rows)]
    turn = jax.random.randint(jax.random.fold_in(own, 2), (rows, 1), 0, top)
    return jnp.take_along_axis(listing, (jnp.arange(top)[None, :] + turn) % top, axis=1)


def portions_of(amount, total, limit, slope, full):
    loads = [(1 << 20) // math.isqrt(grade ** slope) + 1 for grade in range(1, amount + 1)]
    largest = limit if full else min(limit, max(-(-total // amount), total * loads[0] // sum(loads)))
    least = 1 if total - largest >= amount - 1 else 0
    given, surplus = [largest] + [least] * (amount - 1), total - largest - least * (amount - 1)
    while surplus > 0:
        free = [i for i in range(1, amount) if given[i] < largest] or [i for i in range(1, amount) if given[i] < limit]
        mass, budget = sum([loads[i] for i in free]), surplus
        for i in free:
            extra = min(limit - given[i], max(1, budget * loads[i] // mass), surplus)
            given[i] = given[i] + extra
            surplus = surplus - extra
    return np.array(given)


def bell_draw(own_key, extent, scale, reach, split=(), kind=jnp.bfloat16):
    result = scale * jax.random.normal(own_key, extent, jnp.float32)
    if split:
        result = result * level_of(own_key, extent, split, -0.22, 0.18)
    return jnp.clip(result, -reach, reach).astype(kind)


def setup_inputs(seed: int = 0) -> dict:
    arg_keys = jax.random.split(jax.random.key(seed), 7)
    tokens = bell_draw(arg_keys[0], (TOKENS, MODEL_WIDTH), 1.0, 6.0, ((0, 512),))
    base_key_weight = bell_draw(arg_keys[1], (MODEL_WIDTH, KEY_COLUMNS), MODEL_WIDTH ** -0.5, 0.0625, ((1, 16),))
    adapter_down_factors = bell_draw(arg_keys[2], (ADAPTER_COUNT, MODEL_WIDTH, ADAPTER_RANK), MODEL_WIDTH ** -0.5, 0.0625, ((0, 32),))
    adapter_up_factors = bell_draw(arg_keys[3], (ADAPTER_COUNT, ADAPTER_RANK, KEY_COLUMNS), ADAPTER_RANK ** -0.5, 0.75, ((0, 32),))
    token_adapter_index_keys = jax.random.split(jax.random.fold_in(arg_keys[4], 1), TOKENS // TOK_DEV)
    token_adapter_index_turns = jax.random.permutation(jax.random.fold_in(arg_keys[4], 3), TOKENS // TOK_DEV)
    token_adapter_index = jax.vmap(lambda own, number: routed_block(jax.random.fold_in(arg_keys[4], 2), own, number, TOK_DEV, ADAPTER_COUNT, 1, CAP, 1))(token_adapter_index_keys, token_adapter_index_turns).reshape((TOKENS, 1))
    placement = jax.random.permutation(arg_keys[5], ADAPTER_COUNT).astype(jnp.int32)
    return {"tokens": tokens, "base_key_weight": base_key_weight, "adapter_down_factors": adapter_down_factors, "adapter_up_factors": adapter_up_factors, "token_adapter_index": token_adapter_index, "placement": placement}


def reference(tokens, base_key_weight, adapter_down_factors, adapter_up_factors, token_adapter_index, placement):
    adapter_table = adapter_down_factors.shape[0]
    base_out = jnp.dot(tokens, base_key_weight, preferred_element_type=jnp.float32)
    slot_ids = placement[token_adapter_index[:, 0]].astype(jnp.int32)
    num_blocks = TOKENS // TOK_DEV
    block_tokens = tokens.reshape(num_blocks, TOK_DEV, MODEL_WIDTH)
    block_slots = slot_ids.reshape(num_blocks, TOK_DEV)
    gathered_down_factors = adapter_down_factors.astype(jnp.float32)
    gathered_up_factors = adapter_up_factors.astype(jnp.float32)
    columns = jnp.arange(adapter_table, dtype=jnp.int32)

    def per_block(pair_args):
        block_rows, slot_part = pair_args
        dest_hot = (slot_part[:, None] == columns[None, :]).astype(jnp.int32)
        position = jnp.sum(dest_hot * (jnp.cumsum(dest_hot, axis=0) - 1), axis=1)
        flat_index = (slot_part * CAP + position).astype(jnp.int32)
        send_buf = jnp.zeros((adapter_table * CAP, MODEL_WIDTH), jnp.bfloat16).at[flat_index].set(block_rows)
        send_buf = send_buf.reshape(adapter_table, CAP, MODEL_WIDTH).astype(jnp.float32)
        reduced_rank_rows = jnp.einsum('acd,adr->acr', send_buf, gathered_down_factors).astype(jnp.bfloat16)
        adapter_deltas = jnp.einsum('acr,ark->ack', reduced_rank_rows.astype(jnp.float32), gathered_up_factors).astype(jnp.bfloat16)
        return adapter_deltas.reshape(adapter_table * CAP, KEY_COLUMNS)[flat_index]

    adapter_deltas = lax.map(per_block, (block_tokens, block_slots)).reshape(TOKENS, KEY_COLUMNS)
    return (base_out + adapter_deltas.astype(jnp.float32)).astype(jnp.bfloat16)
```

```python
import jax
import jax.numpy as jnp
from jax import lax
from jax.sharding import Mesh, PartitionSpec as P

AXES = ("xl", "y", "xh", "z", "c")
SIZES = (2, 8, 2, 8, 2)
XRING = ("xh", "xl")
f32 = jnp.float32
bf16 = jnp.bfloat16


def pairs_of(move):
    out = []
    for flat in range(512):
        rest, at = flat, []
        for size in reversed(SIZES):
            at.append(rest % size)
            rest //= size
        to = move(*reversed(at))
        index = 0
        for size, place in zip(SIZES, to):
            index = index * size + place % size
        out.append((flat, index))
    return out


def shift(value, axis, by):
    n = lax.axis_size(axis)
    return lax.ppermute(value, axis, [(i, (i + by) % n) for i in range(n)])


def exchange(value, axes):
    return lax.all_to_all(value, axes, split_axis=0, concat_axis=0, tiled=True)


def nt(a, b):
    return lax.dot_general(a, b, (((1,), (1,)), ((), ())), preferred_element_type=f32)


def on_device(tokens, base_key_weight, adapter_down_factors, adapter_up_factors, token_adapter_index, placement):
    rows, width = tokens.shape
    xl, xh, z, c = (lax.axis_index(a) for a in ("xl", "xh", "z", "c"))
    x = 2 * xh + xl
    part = width // 4
    table = placement.shape[0]
    rank = adapter_up_factors.shape[1]
    columns = jnp.arange(table, dtype=jnp.int32)

    id_hot = (token_adapter_index == columns[None, :]).astype(jnp.int32)
    slot_ids = jnp.sum(id_hot * placement[None, :], axis=1)
    slot_row = jnp.tile(slot_ids.astype(bf16)[None, :], (8, part // rows))

    sent = jnp.transpose(tokens.reshape(rows, 4, part), (1, 0, 2))
    sent = jnp.concatenate([sent, jnp.broadcast_to(slot_row[None], (4, 8, part))], axis=1)
    mine = exchange(sent, XRING)
    other = shift(mine, "c", 1)
    x_mine = mine[:, :rows].reshape(4 * rows, part)
    x_other = other[:, :rows].reshape(4 * rows, part)
    ids_mine = mine[:, rows, :rows].reshape(1, 4 * rows)
    ids_other = other[:, rows, :rows].reshape(1, 4 * rows)

    down = adapter_down_factors[0].T
    own = lax.dynamic_slice(down, (0, x * part), (rank, part))
    away = lax.dynamic_slice(down, (0, (3 - x) * part), (rank, part))
    facing = lax.ppermute(away, AXES, pairs_of(lambda xl, y, xh, z, c: (1 - xl, y, 1 - xh, z, c)))
    block = jnp.concatenate([own, facing], axis=0)
    half = rank
    blocks = [(0, block)]
    up_go, dn_go = block, block
    for step in range(1, 4):
        up_go = shift(up_go, "z", 1)
        dn_go = shift(dn_go, "z", -1)
        blocks.append((-step, up_go))
        blocks.append((step, dn_go))
    last = jnp.concatenate([shift(up_go[:half], "z", 1), shift(dn_go[half:], "z", -1)], axis=0)
    blocks.append((4, last))

    panel = base_key_weight.T
    wide = panel.shape[0] // 2
    panel = lax.dynamic_slice(panel, (c * wide, 0), (wide, width))
    to_xl = [lax.dynamic_slice(panel, (0, (2 * xh + d) * part), (wide, part)) for d in range(2)]
    panels = jnp.concatenate([jnp.broadcast_to(p[None], (8, wide, part)) for p in to_xl], axis=0)
    base = exchange(panels, ("xl", "y")).reshape(16 * wide, part)

    up = adapter_up_factors[0].reshape(rank, 4, 4, 2, wide)
    up = lax.dynamic_index_in_dim(up.reshape(rank, 2, 2, 4, 2, wide), xl, 2, keepdims=False)
    up = jnp.transpose(up, (1, 3, 0, 2, 4)).reshape(2, 1, 2, rank, 4 * wide)
    up = jnp.broadcast_to(up, (2, 8, 2, rank, 4 * wide)).reshape(table, rank, 4 * wide)
    up_mine = exchange(up, ("xh", "z", "c")).reshape(table * rank, 4 * wide)
    up_other = shift(up_mine, "c", 1)

    base_mine, base_other = nt(base, x_mine), nt(base, x_other)
    low_mine = jnp.zeros((rank, 4 * rows), f32)
    low_other = jnp.zeros((rank, 4 * rows), f32)
    for off, blk in blocks:
        at = 2 * lax.rem(z + 8 + off, 8) + c
        for side in range(2):
            slot = (at + 16 * (xh if side == 0 else 1 - xh)).astype(bf16)
            w = blk[side * rank:(side + 1) * rank]
            low_mine = low_mine + jnp.where(ids_mine == slot, nt(w, x_mine), 0.0)
            low_other = low_other + jnp.where(ids_other == slot, nt(w, x_other), 0.0)

    def by_core(a, b):
        a, b = a.astype(bf16), b.astype(bf16)
        return jnp.stack([jnp.where(c == 0, a, b), jnp.where(c == 0, b, a)], axis=1)

    base_out = by_core(base_mine.reshape(4, 4 * wide, 4 * rows), base_other.reshape(4, 4 * wide, 4 * rows))
    low_out = by_core(low_mine[None], low_other[None])
    low_out = jnp.broadcast_to(low_out, (4, 2, rank, 4 * rows))
    out = jnp.concatenate([base_out, low_out], axis=2).reshape(8, 4 * wide + rank, 4 * rows)
    got = exchange(out, ("xh", "xl", "c")).reshape(4, 2, 4 * wide + rank, 4 * rows).astype(f32)
    base_sum = jnp.sum(got[:, :, : 4 * wide], axis=0)
    low = jnp.sum(got[:, :, 4 * wide :], axis=(0, 1)).astype(bf16)

    hot = ids_mine == columns.astype(bf16)[:, None]
    spread = jnp.where(hot[:, None, :], low[None], jnp.zeros((), bf16)).reshape(table * rank, 4 * rows)
    tn = lambda a, b: lax.dot_general(a, b, (((0,), (0,)), ((), ())), preferred_element_type=f32)
    d_mine, d_other = tn(up_mine, spread), tn(up_other, spread)
    deltas = jnp.stack([jnp.where(c == 0, d_mine, d_other), jnp.where(c == 0, d_other, d_mine)])
    final = (base_sum + deltas.astype(bf16).astype(f32)).astype(bf16)
    final = jnp.transpose(final.reshape(2, 4, wide, 4, rows), (3, 1, 0, 2, 4)).reshape(4, 8 * wide, rows)
    keys = exchange(final, XRING).reshape(32 * wide, rows)
    return keys.T


def solution(mesh):
    fine = Mesh(mesh.devices.reshape(SIZES), AXES)
    whole = ("xl", "y", "xh", "z", "c")
    adapter = ("xh", "z", "c")
    return jax.shard_map(
        on_device,
        mesh=fine,
        in_specs=(
            P(whole, None),
            P(None, ("xl", "y")),
            P(adapter, None, None),
            P(adapter, None, None),
            P(whole, None),
            P(),
        ),
        out_specs=P(whole, None),
        check_vma=False,
    )
```

```python
import functools

import jax
import jax.numpy as jnp
from jax import lax
from jax.experimental import pallas as pl
from jax.experimental.pallas import tpu as pltpu
from jax.sharding import Mesh, PartitionSpec as P


AXES = ("xl", "y", "xh", "z", "c")
SIZES = (2, 8, 2, 8, 2)
XRING = ("xh", "xl")
LANES = 128
f32 = jnp.float32
bf16 = jnp.bfloat16
i32 = jnp.int32
VMEM = pl.BlockSpec(memory_space=pltpu.VMEM)
SMEM = pl.BlockSpec(memory_space=pltpu.SMEM)


def pairs_of(move):
    out = []
    for flat in range(512):
        rest, at = flat, []
        for size in reversed(SIZES):
            at.append(rest % size)
            rest //= size
        to = move(*reversed(at))
        index = 0
        for size, place in zip(SIZES, to):
            index = index * size + place % size
        out.append((flat, index))
    return out


def shift(value, axis, by):
    n = lax.axis_size(axis)
    return lax.ppermute(value, axis, [(i, (i + by) % n) for i in range(n)])


def exchange(value, axes):
    return lax.all_to_all(value, axes, split_axis=0, concat_axis=0, tiled=True)


def nt(a, b):
    return lax.dot_general(a, b, (((1,), (1,)), ((), ())), preferred_element_type=f32)


def tn(a, b):
    return lax.dot_general(a, b, (((0,), (0,)), ((), ())), preferred_element_type=f32)


def params(mib):
    return pltpu.CompilerParams(vmem_limit_bytes=mib << 20)


def cost(flops, moved):
    return pl.CostEstimate(flops=int(flops), bytes_accessed=int(moved), transcendentals=0)


def pack_kernel(tok, ids, out):
    part = tok.shape[1]
    out[0, :, :part] = tok[...]
    out[0, :, part:] = jnp.broadcast_to(ids[0:1, :], (out.shape[1], LANES))


def pack(tokens, ids):
    rows, width = tokens.shape
    part = width // 4
    return pl.pallas_call(
        pack_kernel,
        grid=(4,),
        in_specs=[
            pl.BlockSpec((rows, part), lambda i: (0, i)),
            pl.BlockSpec((8, LANES), lambda i: (0, 0)),
        ],
        out_specs=pl.BlockSpec((1, rows, part + LANES), lambda i: (i, 0, 0)),
        out_shape=jax.ShapeDtypeStruct((4, rows, part + LANES), bf16),
        cost_estimate=cost(0, 4 * tokens.size),
        compiler_params=params(8),
        name="pack_tokens",
    )(tokens, ids)


def token_rows(ref):
    return ref[:, : ref.shape[1] - LANES]


def token_ids(ref):
    part = ref.shape[1] - LANES
    return jnp.concatenate([ref[s * LANES:s * LANES + 8, part:] for s in range(4)], axis=1)[0:1].astype(f32)


def base_kernel(core, base, mine, other, low, out):
    c = core[0]
    cols = base.shape[0] // 4
    for o, ref in enumerate((mine, other)):
        at = jnp.bitwise_xor(c, o)
        product = nt(base[...], token_rows(ref)).astype(bf16)
        low_rows = low[o].astype(bf16)
        for x in range(4):
            out[2 * x + at, :cols, :] = product[x * cols:(x + 1) * cols]
            out[2 * x + at, cols:, :] = low_rows


def base_product(core, base, mine, other, low):
    cols, part = base.shape
    toks = mine.shape[0]
    return pl.pallas_call(
        base_kernel,
        in_specs=[SMEM, VMEM, VMEM, VMEM, VMEM],
        out_specs=VMEM,
        out_shape=jax.ShapeDtypeStruct((8, cols // 4 + low.shape[1], toks), bf16),
        cost_estimate=cost(4 * cols * part * toks, 2 * (base.size + 2 * mine.size)),
        compiler_params=params(20),
        name="base_product",
    )(core, base, mine, other, low)


def low_kernel(rank, part, slots, *refs):
    count = len(refs) - 5
    blocks, (mine, other, old, new, ups) = refs[:count], refs[count:]
    w = jnp.concatenate([r[:, :part] for r in blocks], axis=0)
    at = 0
    for r in blocks:
        ups[at:at + r.shape[0], :] = r[:, part:]
        at += r.shape[0]
    for o, ref in enumerate((mine, other)):
        product = nt(w, token_rows(ref))
        ids = token_ids(ref)
        total = old[o]
        for a in range(w.shape[0] // rank):
            hit = ids == slots[a].astype(f32)
            total = total + jnp.where(hit, product[a * rank:(a + 1) * rank], 0.0)
        new[o] = total


def low_product(rank, part, slots, blocks, mine, other, old):
    rows = sum(b.shape[0] for b in blocks)
    toks = mine.shape[0]
    lanes = blocks[0].shape[1] - part
    return pl.pallas_call(
        functools.partial(low_kernel, rank, part),
        in_specs=[SMEM] + [VMEM] * (len(blocks) + 3),
        out_specs=[VMEM] * 2,
        out_shape=[jax.ShapeDtypeStruct(old.shape, f32), jax.ShapeDtypeStruct((rows, lanes), bf16)],
        cost_estimate=cost(4 * rows * part * toks, 2 * rows * part),
        compiler_params=params(20),
        name="low_product",
    )(slots, *blocks, mine, other, old)


def final_kernel(rank, wide, slots, got, u_mine, u_other, mine, out):
    toks = got.shape[2]
    quarter = 4 * wide
    base = []
    low = jnp.zeros((rank, toks), f32)
    for c in range(2):
        total = jnp.zeros((quarter, toks), f32)
        for x in range(4):
            total = total + got[2 * x + c, :quarter, :].astype(f32)
            low = low + got[2 * x + c, quarter:, :].astype(f32)
        base.append(total)
    low = low.astype(bf16).astype(f32)
    ids = token_ids(mine)
    delta = None
    for o, u in enumerate((u_mine, u_other)):
        count = u.shape[0] // rank
        spread = jnp.concatenate(
            [jnp.where(ids == slots[o * count + a].astype(f32), low, 0.0) for a in range(count)], axis=0
        ).astype(bf16)
        term = tn(u[...], spread)
        delta = term if delta is None else delta + term
    delta = delta[: 2 * quarter].astype(bf16).astype(f32)
    base = jnp.concatenate([base[c][t * wide:(t + 1) * wide] for t in range(4) for c in range(2)], axis=0)
    keys = (base + delta).astype(bf16)
    rows = toks // 4
    for x in range(4):
        out[x] = keys[:, x * rows:(x + 1) * rows]


def finish(rank, wide, slots, got, u_mine, u_other, mine):
    toks = got.shape[2]
    return pl.pallas_call(
        functools.partial(final_kernel, rank, wide),
        in_specs=[SMEM] + [VMEM] * 4,
        out_specs=VMEM,
        out_shape=jax.ShapeDtypeStruct((4, 8 * wide, toks // 4), bf16),
        cost_estimate=cost(4 * u_mine.size * toks, 2 * got.size),
        compiler_params=params(20),
        name="finish",
    )(slots, got, u_mine, u_other, mine)


def on_device(tokens, base_key_weight, adapter_down_factors, adapter_up_factors, token_adapter_index, placement):
    rows, width = tokens.shape
    xl, xh, z, c = (lax.axis_index(a) for a in ("xl", "xh", "z", "c"))
    x = 2 * xh + xl
    part = width // 4
    table = placement.shape[0]
    rank = adapter_up_factors.shape[1]
    key_part = adapter_up_factors.shape[2] // 4
    columns = jnp.arange(table, dtype=i32)
    core = c.astype(i32).reshape(1)

    down = adapter_down_factors[0].T
    up = adapter_up_factors[0]
    pad = -key_part % LANES

    def factor_slice(at):
        d = lax.dynamic_slice(down, (0, at * part), (rank, part))
        u = lax.dynamic_slice(up, (0, at * key_part), (rank, key_part))
        return jnp.concatenate([d, jnp.pad(u, ((0, 0), (0, pad)))], axis=1)

    own = factor_slice(x)
    facing = lax.ppermute(
        factor_slice(3 - x), AXES, pairs_of(lambda xl, y, xh, z, c: (1 - xl, y, 1 - xh, z, c))
    )
    ring = pairs_of(lambda xl, y, xh, z, c: (xl, y, xh, z + 1 - 2 * c, c))
    a = jnp.concatenate([own, shift(own, "c", 1)], axis=0)
    b = jnp.concatenate([facing, shift(facing, "c", 1)], axis=0)
    held = [own, facing]
    for step in range(1, 5):
        a = lax.ppermute(a if step < 4 else a[:rank], AXES, ring)
        b = lax.ppermute(b if step < 4 else b[:rank], AXES, ring)
        held += [a, b]

    id_hot = (token_adapter_index == columns[None, :]).astype(i32)
    slot_ids = jnp.sum(id_hot * placement[None, :], axis=1)
    id_rows = jnp.broadcast_to(slot_ids.astype(bf16)[None, :], (8, rows))
    packed = pack(tokens, id_rows)
    mine = exchange(packed, XRING).reshape(4 * rows, part + LANES)
    other = shift(mine, "c", 1)

    panel = base_key_weight.T
    wide = panel.shape[0] // 2
    panel = lax.dynamic_slice(panel, (c * wide, 0), (wide, width))
    to_xl = [lax.dynamic_slice(panel, (0, (2 * xh + d) * part), (wide, part)) for d in range(2)]
    panels = jnp.concatenate([jnp.broadcast_to(p[None], (8, wide, part)) for p in to_xl], axis=0)
    base = exchange(panels, ("xl", "y")).reshape(16 * wide, part)

    def slot_list(cc):
        def at(side, off, core_at):
            return 16 * (xh if side == 0 else 1 - xh) + 2 * jnp.bitwise_and(z + off + 8, 7) + core_at

        out = [at(0, 0, cc), at(1, 0, cc)]
        for step in range(1, 4):
            off = step * (2 * cc - 1)
            for side in range(2):
                out += [at(side, off, cc), at(side, off, 1 - cc)]
        return jnp.stack(out + [at(0, 4, cc), at(1, 4, cc)]).astype(i32)

    slots_mine, slots_other = slot_list(c), slot_list(1 - c)
    low = jnp.zeros((2, rank, 4 * rows), f32)
    ups = []
    for k, (first, end) in enumerate(((0, 3), (3, 5), (5, 7), (7, 10))):
        low, u = low_product(rank, part, slots_mine[4 * k:4 * k + 4], held[first:end], mine, other, low)
        ups.append(u)
    u_mine = jnp.concatenate(ups, axis=0)
    u_other = shift(u_mine, "c", 1)

    out = base_product(core, base, mine, other, low)
    got = exchange(out, ("xh", "xl", "c"))
    slots = jnp.concatenate([slots_mine, slots_other])
    keys = exchange(finish(rank, wide, slots, got, u_mine, u_other, mine), XRING)
    return keys.reshape(32 * wide, rows).T


def solution(mesh):
    fine = Mesh(mesh.devices.reshape(SIZES), AXES)
    whole = ("xl", "y", "xh", "z", "c")
    adapter = ("xh", "z", "c")

    return jax.shard_map(
        on_device,
        mesh=fine,
        in_specs=(
            P(whole, None),
            P(None, ("xl", "y")),
            P(adapter, None, None),
            P(adapter, None, None),
            P(whole, None),
            P(),
        ),
        out_specs=P(whole, None),
        check_vma=False,
    )
```

```python
import functools

import jax
import jax.numpy as jnp
from jax import lax
from jax.experimental import pallas as pl
from jax.experimental.pallas import tpu as pltpu
from jax.sharding import Mesh, PartitionSpec as P


AXES = ("xl", "y", "xh", "z", "c")
SIZES = (2, 8, 2, 8, 2)
XRING = ("xh", "xl")
LANES = 128
f32 = jnp.float32
bf16 = jnp.bfloat16
i32 = jnp.int32
VMEM = pl.BlockSpec(memory_space=pltpu.VMEM)
SMEM = pl.BlockSpec(memory_space=pltpu.SMEM)


def pairs_of(move):
    out = []
    for flat in range(512):
        rest, at = flat, []
        for size in reversed(SIZES):
            at.append(rest % size)
            rest //= size
        to = move(*reversed(at))
        index = 0
        for size, place in zip(SIZES, to):
            index = index * size + place % size
        out.append((flat, index))
    return out


def shift(value, axis, by):
    n = lax.axis_size(axis)
    return lax.ppermute(value, axis, [(i, (i + by) % n) for i in range(n)])


def exchange(value, axes):
    return lax.all_to_all(value, axes, split_axis=0, concat_axis=0, tiled=True)


def nt(a, b):
    return lax.dot_general(a, b, (((1,), (1,)), ((), ())), preferred_element_type=f32)


def params(mib):
    return pltpu.CompilerParams(vmem_limit_bytes=mib << 20)


def cost(flops, moved):
    return pl.CostEstimate(flops=int(flops), bytes_accessed=int(moved), transcendentals=0)


def pack_kernel(tok, ids, out):
    part = tok.shape[1]
    out[0, :, :part] = tok[...]
    out[0, :, part:] = jnp.broadcast_to(ids[0:1, :], (out.shape[1], LANES))


def pack(tokens, ids):
    rows, width = tokens.shape
    part = width // 4
    return pl.pallas_call(
        pack_kernel,
        grid=(4,),
        in_specs=[
            pl.BlockSpec((rows, part), lambda i: (0, i)),
            pl.BlockSpec((8, LANES), lambda i: (0, 0)),
        ],
        out_specs=pl.BlockSpec((1, rows, part + LANES), lambda i: (i, 0, 0)),
        out_shape=jax.ShapeDtypeStruct((4, rows, part + LANES), bf16),
        cost_estimate=cost(0, 4 * tokens.size),
        compiler_params=params(8),
        name="pack_tokens",
    )(tokens, ids)


HELD = [(0, 0, 0), (1, 0, 0)]
HELD += [(side, step, flip) for step in (1, 2, 3) for side in (0, 1) for flip in (0, 1)]
HELD += [(0, 4, 0), (1, 4, 0)]


def slot_of(place, entry, core):
    side, step, flip = entry
    xh, z = place[2], place[3]
    line = jnp.bitwise_and(z + step * (2 * core - 1) + 8, 7)
    return (16 * (1 - xh if side else xh) + 2 * line + (1 - core if flip else core)).astype(f32)


def factors_kernel(place, down, up, own, away):
    part = own.shape[1] - up.shape[1]
    for at, out in ((place[0], own), (3 - place[0], away)):
        out[:, :part] = down[:, pl.ds(pl.multiple_of(at * part, LANES), part)]
        out[:, part:] = up[...]


def factors(place, down, up):
    rank, width = down.shape
    piece = jax.ShapeDtypeStruct((rank, width // 4 + up.shape[1]), bf16)
    return pl.pallas_call(
        factors_kernel,
        in_specs=[SMEM, VMEM, VMEM],
        out_specs=[VMEM] * 2,
        out_shape=[piece] * 2,
        cost_estimate=cost(0, 4 * down.size),
        compiler_params=params(6),
        name="factors",
    )(place, down, up)


def panels_kernel(place, panel, out):
    wide, part = out.shape[1:]
    for d in range(2):
        at = pl.multiple_of((2 * place[2] + d) * part, LANES)
        both = panel[:, pl.ds(at, part)]
        rows = jnp.where(place[4] == 0, both[:wide], both[wide:])
        for y in range(8):
            out[8 * d + y] = rows


def spread_panels(place, panel):
    wide, part = panel.shape[0] // 2, panel.shape[1] // 4
    return pl.pallas_call(
        panels_kernel,
        in_specs=[SMEM, VMEM],
        out_specs=VMEM,
        out_shape=jax.ShapeDtypeStruct((16, wide, part), bf16),
        cost_estimate=cost(0, 40 * wide * part),
        compiler_params=params(6),
        name="spread_panels",
    )(place, panel)


def head_kernel(ref, out):
    out[...] = ref[0:out.shape[0], :]


def head(value, rows):
    return pl.pallas_call(
        head_kernel,
        in_specs=[VMEM],
        out_specs=VMEM,
        out_shape=jax.ShapeDtypeStruct((rows, value.shape[1]), value.dtype),
        cost_estimate=cost(0, 4 * rows * value.shape[1]),
        compiler_params=params(4),
        name="head",
    )(value)


def join_kernel(*refs):
    out, at = refs[-1], 0
    for ref in refs[:-1]:
        out[at:at + ref.shape[0], :] = ref[...]
        at += ref.shape[0]


def join(parts):
    rows = sum(p.shape[0] for p in parts)
    return pl.pallas_call(
        join_kernel,
        in_specs=[VMEM] * len(parts),
        out_specs=VMEM,
        out_shape=jax.ShapeDtypeStruct((rows, parts[0].shape[1]), parts[0].dtype),
        cost_estimate=cost(0, 4 * rows * parts[0].shape[1]),
        compiler_params=params(6),
        name="join",
    )(*parts)


def token_rows(ref):
    return ref[:, : ref.shape[1] - LANES]


def token_ids(ref):
    part = ref.shape[1] - LANES
    return jnp.concatenate([ref[s * LANES:s * LANES + 8, part:] for s in range(4)], axis=1)[0:1].astype(f32)


def base_kernel(place, base, mine, other, low, out):
    cols, rows = base.shape[0], out.shape[2]
    out[:, cols:, :] = low[...]
    for o, ref in enumerate((mine, other)):
        at = jnp.bitwise_xor(place[4], o)
        product = nt(base[...], token_rows(ref)).astype(bf16)
        for x in range(4):
            out[2 * x + at, :cols, :] = product[:, x * rows:(x + 1) * rows]


def base_product(place, base, mine, other, low):
    cols, part = base.shape
    toks = mine.shape[0]
    return pl.pallas_call(
        base_kernel,
        in_specs=[SMEM] + [VMEM] * 4,
        out_specs=VMEM,
        out_shape=jax.ShapeDtypeStruct((8, cols + low.shape[1], toks // 4), bf16),
        cost_estimate=cost(4 * cols * part * toks, 2 * (base.size + 2 * mine.size)),
        compiler_params=params(20),
        name="base_product",
    )(place, base, mine, other, low)


def low_kernel(rank, part, entries, last, place, *refs):
    count = len(refs) - 4 - last
    blocks, (mine, other) = refs[:count], refs[count:count + 2]
    new, ups = refs[-2:]
    w = jnp.concatenate([r[:, :part] for r in blocks], axis=0)
    at = 0
    for r in blocks:
        ups[at:at + r.shape[0], :] = r[:, part:]
        at += r.shape[0]
    for o, ref in enumerate((mine, other)):
        product = nt(w, token_rows(ref))
        ids = token_ids(ref)
        total = refs[count + 2][o] if last else jnp.zeros(new.shape[1:], f32)
        for a, entry in enumerate(entries):
            hit = ids == slot_of(place, entry, place[4])
            total = total + jnp.where(hit, product[a * rank:(a + 1) * rank], 0.0)
        if last:
            sent, rows = total.astype(bf16), new.shape[2]
            for x in range(4):
                new[2 * x + jnp.bitwise_xor(place[4], o)] = sent[:, x * rows:(x + 1) * rows]
        else:
            new[o] = total


def low_product(rank, part, entries, place, blocks, mine, other, old=None):
    rows = sum(b.shape[0] for b in blocks)
    toks = mine.shape[0]
    lanes = blocks[0].shape[1] - part
    last = old is not None
    if last:
        result = jax.ShapeDtypeStruct((8, rank, toks // 4), bf16)
    else:
        result = jax.ShapeDtypeStruct((2, rank, toks), f32)
    operands = (*blocks, mine, other) + ((old,) if last else ())
    return pl.pallas_call(
        functools.partial(low_kernel, rank, part, entries, last),
        in_specs=[SMEM] + [VMEM] * len(operands),
        out_specs=[VMEM] * 2,
        out_shape=[result, jax.ShapeDtypeStruct((rows, lanes), bf16)],
        cost_estimate=cost(4 * rows * part * toks, 2 * rows * part),
        compiler_params=params(20),
        name="low_product",
    )(place, *operands)


def final_kernel(rank, wide, place, got, u_mine0, u_mine1, u_other0, u_other1, ids, out):
    rows = got.shape[2]
    cols = got.shape[1] - rank
    base = []
    low = jnp.zeros((rank, rows), f32)
    for c in range(2):
        total = jnp.zeros((cols, rows), f32)
        for x in range(4):
            total = total + got[2 * x + c, :cols, :].astype(f32)
            low = low + got[2 * x + c, cols:, :].astype(f32)
        base.append(total)
    base = jnp.concatenate(
        [base[c][t * wide:(t + 1) * wide] for t in range(cols // wide) for c in range(2)], axis=0
    )
    low = low.astype(bf16).astype(f32)
    names = ids[0:1, :].astype(f32)
    delta = None
    for o, k, u in ((0, 0, u_mine0), (1, 0, u_other0), (0, 1, u_mine1), (1, 1, u_other1)):
        core = 1 - place[4] if o else place[4]
        entries = HELD[8 * k:8 * k + 8]
        spread = jnp.concatenate(
            [jnp.where(names == slot_of(place, entry, core), low, 0.0) for entry in entries], axis=0
        )
        term = jnp.dot(spread.T.astype(bf16), u[...], preferred_element_type=f32)
        delta = term if delta is None else delta + term
    out[...] = (base.T + delta.astype(bf16).astype(f32)).astype(bf16)


def finish(rank, wide, place, got, ups, ids):
    rows = got.shape[2]
    return pl.pallas_call(
        functools.partial(final_kernel, rank, wide),
        in_specs=[SMEM] + [VMEM] * 6,
        out_specs=VMEM,
        out_shape=jax.ShapeDtypeStruct((rows, 2 * (got.shape[1] - rank)), bf16),
        cost_estimate=cost(8 * ups[0].size * rows, 2 * got.size),
        compiler_params=params(20),
        name="finish",
    )(place, got, *ups, ids)


def on_device(tokens, base_key_weight, adapter_down_factors, adapter_up_factors, token_adapter_index, placement):
    rows, width = tokens.shape
    xl, xh, z, c = (lax.axis_index(a) for a in ("xl", "xh", "z", "c"))
    x = 2 * xh + xl
    part = width // 4
    table = placement.shape[0]
    rank = adapter_up_factors.shape[1]
    columns = jnp.arange(table, dtype=i32)
    place = jnp.stack([x, 1 - 2 * c, xh, z, c]).astype(i32)

    own, away = factors(place, adapter_down_factors[0].T, adapter_up_factors[0])
    facing = lax.ppermute(away, AXES, pairs_of(lambda xl, y, xh, z, c: (1 - xl, y, 1 - xh, z, c)))
    ring = pairs_of(lambda xl, y, xh, z, c: (xl, y, xh, z + 1 - 2 * c, c))
    a = join([own, shift(own, "c", 1)])
    b = join([facing, shift(facing, "c", 1)])
    held = [own, facing]
    for step in range(1, 5):
        a = lax.ppermute(a if step < 4 else head(a, rank), AXES, ring)
        b = lax.ppermute(b if step < 4 else head(b, rank), AXES, ring)
        held += [a, b]

    id_hot = (token_adapter_index == columns[None, :]).astype(i32)
    slot_ids = jnp.sum(id_hot * placement[None, :], axis=1)
    id_rows = jnp.broadcast_to(slot_ids.astype(bf16)[None, :], (8, rows))
    packed = pack(tokens, id_rows)
    mine = exchange(packed, XRING).reshape(4 * rows, part + LANES)
    other = shift(mine, "c", 1)

    panels = spread_panels(place, base_key_weight.T)
    wide = panels.shape[1]
    base = exchange(panels, ("xl", "y")).reshape(16 * wide, part)

    low, up_first = low_product(rank, part, HELD[:8], place, held[:5], mine, other)
    low, up_second = low_product(rank, part, HELD[8:], place, held[5:], mine, other, low)
    out = base_product(place, base, mine, other, low)
    got = exchange(out, ("xh", "xl", "c"))
    other_first = shift(up_first, "c", 1)
    other_second = shift(up_second, "c", 1)
    ups = (up_first, up_second, other_first, other_second)
    return finish(rank, wide, place, got, ups, id_rows)


def solution(mesh):
    fine = Mesh(mesh.devices.reshape(SIZES), AXES)
    whole = ("xl", "y", "xh", "z", "c")
    adapter = ("xh", "z", "c")

    return jax.shard_map(
        on_device,
        mesh=fine,
        in_specs=(
            P(whole, None),
            P(None, ("xl", "y")),
            P(adapter, None, None),
            P(adapter, None, None),
            P(whole, None),
            P(),
        ),
        out_specs=P(whole, None),
        check_vma=False,
    )
```

```python
import functools

import jax
import jax.numpy as jnp
from jax import lax
from jax.experimental import pallas as pl
from jax.experimental.pallas import tpu as pltpu
from jax.sharding import Mesh, PartitionSpec as P


AXES = ("xl", "y", "xh", "z", "c")
SIZES = (2, 8, 2, 8, 2)
XRING = ("xh", "xl")
LANES = 128
f32 = jnp.float32
bf16 = jnp.bfloat16
i32 = jnp.int32
VMEM = pl.BlockSpec(memory_space=pltpu.VMEM)
SMEM = pl.BlockSpec(memory_space=pltpu.SMEM)
HBM = pl.BlockSpec(memory_space=pltpu.HBM)


def pairs_of(move):
    out = []
    for flat in range(512):
        rest, at = flat, []
        for size in reversed(SIZES):
            at.append(rest % size)
            rest //= size
        to = move(*reversed(at))
        index = 0
        for size, place in zip(SIZES, to):
            index = index * size + place % size
        out.append((flat, index))
    return out


def shift(value, axis, by):
    n = lax.axis_size(axis)
    return lax.ppermute(value, axis, [(i, (i + by) % n) for i in range(n)])


def exchange(value, axes):
    return lax.all_to_all(value, axes, split_axis=0, concat_axis=0, tiled=True)


def nt(a, b):
    return lax.dot_general(a, b, (((1,), (1,)), ((), ())), preferred_element_type=f32)


def params(mib):
    return pltpu.CompilerParams(vmem_limit_bytes=mib << 20)


def cost(flops, moved):
    return pl.CostEstimate(flops=int(flops), bytes_accessed=int(moved), transcendentals=0)


def pack_kernel(tok, ids, out):
    part = tok.shape[1]
    out[0, :, :part] = tok[...]
    out[0, :, part:] = jnp.broadcast_to(ids[0:1, :], (out.shape[1], LANES))


def pack(tokens, ids):
    rows, width = tokens.shape
    part = width // 4
    return pl.pallas_call(
        pack_kernel,
        grid=(4,),
        in_specs=[
            pl.BlockSpec((rows, part), lambda i: (0, i)),
            pl.BlockSpec((8, LANES), lambda i: (0, 0)),
        ],
        out_specs=pl.BlockSpec((1, rows, part + LANES), lambda i: (i, 0, 0)),
        out_shape=jax.ShapeDtypeStruct((4, rows, part + LANES), bf16),
        cost_estimate=cost(0, 4 * tokens.size),
        compiler_params=params(8),
        name="pack_tokens",
    )(tokens, ids)


HELD = [(0, 0, 0), (1, 0, 0)]
HELD += [(side, step, flip) for step in (1, 2, 3) for side in (0, 1) for flip in (0, 1)]
HELD += [(0, 4, 0), (1, 4, 0)]


def slot_of(place, entry, core):
    side, step, flip = entry
    xh, z = place[2], place[3]
    line = jnp.bitwise_and(z + step * (2 * core - 1) + 8, 7)
    return (16 * (1 - xh if side else xh) + 2 * line + (1 - core if flip else core)).astype(f32)


def factors_kernel(place, down, up, own, away):
    part = own.shape[1] - up.shape[1]
    for at, out in ((place[0], own), (3 - place[0], away)):
        out[:, :part] = down[:, pl.ds(pl.multiple_of(at * part, LANES), part)]
        out[:, part:] = up[...]


def factors(place, down, up):
    rank, width = down.shape
    piece = jax.ShapeDtypeStruct((rank, width // 4 + up.shape[1]), bf16)
    return pl.pallas_call(
        factors_kernel,
        in_specs=[SMEM, VMEM, VMEM],
        out_specs=[VMEM] * 2,
        out_shape=[piece] * 2,
        cost_estimate=cost(0, 4 * down.size),
        compiler_params=params(6),
        name="factors",
    )(place, down, up)


def panels_kernel(place, panel, out):
    wide, part = out.shape[1:]
    for d in range(2):
        at = pl.multiple_of((2 * place[2] + d) * part, LANES)
        both = panel[:, pl.ds(at, part)]
        rows = jnp.where(place[4] == 0, both[:wide], both[wide:])
        for y in range(8):
            out[8 * d + y] = rows


def spread_panels(place, panel):
    wide, part = panel.shape[0] // 2, panel.shape[1] // 4
    return pl.pallas_call(
        panels_kernel,
        in_specs=[SMEM, VMEM],
        out_specs=VMEM,
        out_shape=jax.ShapeDtypeStruct((16, wide, part), bf16),
        cost_estimate=cost(0, 40 * wide * part),
        compiler_params=params(6),
        name="spread_panels",
    )(place, panel)


def head_kernel(ref, out):
    out[...] = ref[0:out.shape[0], :]


def head(value, rows):
    return pl.pallas_call(
        head_kernel,
        in_specs=[VMEM],
        out_specs=VMEM,
        out_shape=jax.ShapeDtypeStruct((rows, value.shape[1]), value.dtype),
        cost_estimate=cost(0, 4 * rows * value.shape[1]),
        compiler_params=params(4),
        name="head",
    )(value)


def join_kernel(*refs):
    out, at = refs[-1], 0
    for ref in refs[:-1]:
        out[at:at + ref.shape[0], :] = ref[...]
        at += ref.shape[0]


def join(parts):
    rows = sum(p.shape[0] for p in parts)
    return pl.pallas_call(
        join_kernel,
        in_specs=[VMEM] * len(parts),
        out_specs=VMEM,
        out_shape=jax.ShapeDtypeStruct((rows, parts[0].shape[1]), parts[0].dtype),
        cost_estimate=cost(0, 4 * rows * parts[0].shape[1]),
        compiler_params=params(6),
        name="join",
    )(*parts)


def token_rows(ref):
    return ref[:, : ref.shape[1] - LANES]


def token_ids(ref):
    part = ref.shape[1] - LANES
    return jnp.concatenate([ref[s * LANES:s * LANES + 8, part:] for s in range(4)], axis=1)[0:1].astype(f32)


def base_kernel(place, base, mine, other, low, out, near, sem):
    cols, rows = base.shape[0], out.shape[2]
    copy = pltpu.make_async_copy(mine, near, sem)
    copy.start()
    out[:, cols:, :] = low[...]
    for o, ref in ((1, other), (0, near)):
        if o == 0:
            copy.wait()
        at = jnp.bitwise_xor(place[4], o)
        product = nt(base[...], token_rows(ref)).astype(bf16)
        for x in range(4):
            out[2 * x + at, :cols, :] = product[:, x * rows:(x + 1) * rows]


def base_product(place, base, mine, other, low):
    cols, part = base.shape
    toks = mine.shape[0]
    return pl.pallas_call(
        base_kernel,
        in_specs=[SMEM, VMEM, HBM, VMEM, VMEM],
        out_specs=VMEM,
        out_shape=jax.ShapeDtypeStruct((8, cols + low.shape[1], toks // 4), bf16),
        scratch_shapes=[pltpu.VMEM(mine.shape, bf16), pltpu.SemaphoreType.DMA(())],
        cost_estimate=cost(4 * cols * part * toks, 2 * (base.size + 2 * mine.size)),
        compiler_params=params(20),
        name="base_product",
    )(place, base, mine, other, low)


def low_kernel(rank, part, entries, last, place, *refs):
    count = len(refs) - 4 - last
    blocks, (mine, other) = refs[:count], refs[count:count + 2]
    new, ups = refs[-2:]
    w = jnp.concatenate([r[:, :part] for r in blocks], axis=0)
    at = 0
    for r in blocks:
        ups[at:at + r.shape[0], :] = r[:, part:]
        at += r.shape[0]
    for o, ref in enumerate((mine, other)):
        product = nt(w, token_rows(ref))
        ids = token_ids(ref)
        total = refs[count + 2][o] if last else jnp.zeros(new.shape[1:], f32)
        for a, entry in enumerate(entries):
            hit = ids == slot_of(place, entry, place[4])
            total = total + jnp.where(hit, product[a * rank:(a + 1) * rank], 0.0)
        if last:
            sent, rows = total.astype(bf16), new.shape[2]
            for x in range(4):
                new[2 * x + jnp.bitwise_xor(place[4], o)] = sent[:, x * rows:(x + 1) * rows]
        else:
            new[o] = total


def low_product(rank, part, entries, place, blocks, mine, other, old=None):
    rows = sum(b.shape[0] for b in blocks)
    toks = mine.shape[0]
    lanes = blocks[0].shape[1] - part
    last = old is not None
    if last:
        result = jax.ShapeDtypeStruct((8, rank, toks // 4), bf16)
    else:
        result = jax.ShapeDtypeStruct((2, rank, toks), f32)
    operands = (*blocks, mine, other) + ((old,) if last else ())
    return pl.pallas_call(
        functools.partial(low_kernel, rank, part, entries, last),
        in_specs=[SMEM] + [VMEM] * len(operands),
        out_specs=[VMEM] * 2,
        out_shape=[result, jax.ShapeDtypeStruct((rows, lanes), bf16)],
        cost_estimate=cost(4 * rows * part * toks, 2 * rows * part),
        compiler_params=params(20),
        name="low_product",
    )(place, *operands)


def final_kernel(rank, wide, place, got, u_mine0, u_mine1, u_other0, u_other1, ids, out, near, sems):
    order = ((0, 0, u_mine0), (1, 0, u_other0), (0, 1, u_mine1), (1, 1, u_other1))
    copies = [pltpu.make_async_copy(u, near.at[i], sems.at[i]) for i, (_, _, u) in enumerate(order)]
    for copy in copies:
        copy.start()
    rows = got.shape[2]
    cols = got.shape[1] - rank
    base = []
    low = jnp.zeros((rank, rows), f32)
    for c in range(2):
        total = jnp.zeros((cols, rows), f32)
        for x in range(4):
            total = total + got[2 * x + c, :cols, :].astype(f32)
            low = low + got[2 * x + c, cols:, :].astype(f32)
        base.append(total)
    base = jnp.concatenate(
        [base[c][t * wide:(t + 1) * wide] for t in range(cols // wide) for c in range(2)], axis=0
    )
    low = low.astype(bf16).astype(f32)
    names = ids[0:1, :].astype(f32)
    delta = None
    for i, (o, k, _) in enumerate(order):
        core = 1 - place[4] if o else place[4]
        entries = HELD[8 * k:8 * k + 8]
        spread = jnp.concatenate(
            [jnp.where(names == slot_of(place, entry, core), low, 0.0) for entry in entries], axis=0
        )
        copies[i].wait()
        term = jnp.dot(spread.T.astype(bf16), near[i], preferred_element_type=f32)
        delta = term if delta is None else delta + term
    out[...] = (base.T + delta.astype(bf16).astype(f32)).astype(bf16)


def finish(rank, wide, place, got, ups, ids):
    rows = got.shape[2]
    return pl.pallas_call(
        functools.partial(final_kernel, rank, wide),
        in_specs=[SMEM, VMEM] + [HBM] * 4 + [VMEM],
        out_specs=VMEM,
        scratch_shapes=[pltpu.VMEM((4,) + ups[0].shape, bf16), pltpu.SemaphoreType.DMA((4,))],
        out_shape=jax.ShapeDtypeStruct((rows, 2 * (got.shape[1] - rank)), bf16),
        cost_estimate=cost(8 * ups[0].size * rows, 2 * got.size),
        compiler_params=params(58),
        name="finish",
    )(place, got, *ups, ids)


def on_device(tokens, base_key_weight, adapter_down_factors, adapter_up_factors, token_adapter_index, placement):
    rows, width = tokens.shape
    xl, xh, z, c = (lax.axis_index(a) for a in ("xl", "xh", "z", "c"))
    x = 2 * xh + xl
    part = width // 4
    table = placement.shape[0]
    rank = adapter_up_factors.shape[1]
    columns = jnp.arange(table, dtype=i32)
    place = jnp.stack([x, 1 - 2 * c, xh, z, c]).astype(i32)

    own, away = factors(place, adapter_down_factors[0].T, adapter_up_factors[0])
    facing = lax.ppermute(away, AXES, pairs_of(lambda xl, y, xh, z, c: (1 - xl, y, 1 - xh, z, c)))
    ring = pairs_of(lambda xl, y, xh, z, c: (xl, y, xh, z + 1 - 2 * c, c))
    a = join([own, shift(own, "c", 1)])
    b = join([facing, shift(facing, "c", 1)])
    held = [own, facing]
    for step in range(1, 5):
        a = lax.ppermute(a if step < 4 else head(a, rank), AXES, ring)
        b = lax.ppermute(b if step < 4 else head(b, rank), AXES, ring)
        held += [a, b]

    id_hot = (token_adapter_index == columns[None, :]).astype(i32)
    slot_ids = jnp.sum(id_hot * placement[None, :], axis=1)
    id_rows = jnp.broadcast_to(slot_ids.astype(bf16)[None, :], (8, rows))
    packed = pack(tokens, id_rows)
    mine = exchange(packed, XRING).reshape(4 * rows, part + LANES)
    other = shift(mine, "c", 1)

    panels = spread_panels(place, base_key_weight.T)
    wide = panels.shape[1]
    base = exchange(panels, ("xl", "y")).reshape(16 * wide, part)

    low, up_first = low_product(rank, part, HELD[:8], place, held[:5], mine, other)
    low, up_second = low_product(rank, part, HELD[8:], place, held[5:], mine, other, low)
    out = base_product(place, base, mine, other, low)
    got = exchange(out, ("xh", "xl", "c"))
    other_first = shift(up_first, "c", 1)
    other_second = shift(up_second, "c", 1)
    ups = (up_first, up_second, other_first, other_second)
    return finish(rank, wide, place, got, ups, id_rows)


def solution(mesh):
    fine = Mesh(mesh.devices.reshape(SIZES), AXES)
    whole = ("xl", "y", "xh", "z", "c")
    adapter = ("xh", "z", "c")

    return jax.shard_map(
        on_device,
        mesh=fine,
        in_specs=(
            P(whole, None),
            P(None, ("xl", "y")),
            P(adapter, None, None),
            P(adapter, None, None),
            P(whole, None),
            P(),
        ),
        out_specs=P(whole, None),
        check_vma=False,
    )
```

```python
import functools

import jax
import jax.numpy as jnp
from jax import lax
from jax.experimental import pallas as pl
from jax.experimental.pallas import tpu as pltpu
from jax.sharding import Mesh, PartitionSpec as P


AXES = ("xl", "y", "xh", "z", "c")
SIZES = (2, 8, 2, 8, 2)
XRING = ("xh", "xl")
LANES = 128
f32 = jnp.float32
bf16 = jnp.bfloat16
i32 = jnp.int32
VMEM = pl.BlockSpec(memory_space=pltpu.VMEM)
SMEM = pl.BlockSpec(memory_space=pltpu.SMEM)


def pairs_of(move):
    out = []
    for flat in range(512):
        rest, at = flat, []
        for size in reversed(SIZES):
            at.append(rest % size)
            rest //= size
        to = move(*reversed(at))
        index = 0
        for size, place in zip(SIZES, to):
            index = index * size + place % size
        out.append((flat, index))
    return out


def shift(value, axis, by):
    n = lax.axis_size(axis)
    return lax.ppermute(value, axis, [(i, (i + by) % n) for i in range(n)])


def exchange(value, axes):
    return lax.all_to_all(value, axes, split_axis=0, concat_axis=0, tiled=True)


def nt(a, b):
    return lax.dot_general(a, b, (((1,), (1,)), ((), ())), preferred_element_type=f32)


def params(mib):
    return pltpu.CompilerParams(vmem_limit_bytes=mib << 20)


def cost(flops, moved):
    return pl.CostEstimate(flops=int(flops), bytes_accessed=int(moved), transcendentals=0)


def pack_kernel(tok, ids, out):
    part = tok.shape[1]
    out[0, :, :part] = tok[...]
    out[0, :, part:] = jnp.broadcast_to(ids[0:1, :], (out.shape[1], LANES))


def pack(tokens, ids):
    rows, width = tokens.shape
    part = width // 4
    return pl.pallas_call(
        pack_kernel,
        grid=(4,),
        in_specs=[
            pl.BlockSpec((rows, part), lambda i: (0, i)),
            pl.BlockSpec((8, LANES), lambda i: (0, 0)),
        ],
        out_specs=pl.BlockSpec((1, rows, part + LANES), lambda i: (i, 0, 0)),
        out_shape=jax.ShapeDtypeStruct((4, rows, part + LANES), bf16),
        cost_estimate=cost(0, 4 * tokens.size),
        compiler_params=params(8),
        name="pack_tokens",
    )(tokens, ids)


def join_kernel(*refs):
    out, at = refs[-1], 0
    for ref in refs[:-1]:
        out[at:at + ref.shape[0], :] = ref[...]
        at += ref.shape[0]


def join(parts):
    rows = sum(p.shape[0] for p in parts)
    return pl.pallas_call(
        join_kernel,
        in_specs=[VMEM] * len(parts),
        out_specs=VMEM,
        out_shape=jax.ShapeDtypeStruct((rows, parts[0].shape[1]), parts[0].dtype),
        cost_estimate=cost(0, 4 * rows * parts[0].shape[1]),
        compiler_params=params(6),
        name="join",
    )(*parts)


def token_rows(ref):
    return ref[:, : ref.shape[1] - LANES]


def token_ids(ref):
    part = ref.shape[1] - LANES
    return jnp.concatenate([ref[s * LANES:s * LANES + 8, part:] for s in range(4)], axis=1)[0:1].astype(f32)


def base_kernel(core, base, mine, other, low, out):
    cols = base.shape[0]
    rows = out.shape[2]
    for o, ref in enumerate((mine, other)):
        at = jnp.bitwise_xor(core[0], o)
        product = nt(base[...], token_rows(ref)).astype(bf16)
        low_rows = low[o].astype(bf16)
        for x in range(4):
            out[2 * x + at, :cols, :] = product[:, x * rows:(x + 1) * rows]
            out[2 * x + at, cols:, :] = low_rows[:, x * rows:(x + 1) * rows]


def base_product(core, base, mine, other, low):
    cols, part = base.shape
    toks = mine.shape[0]
    return pl.pallas_call(
        base_kernel,
        in_specs=[SMEM, VMEM, VMEM, VMEM, VMEM],
        out_specs=VMEM,
        out_shape=jax.ShapeDtypeStruct((8, cols + low.shape[1], toks // 4), bf16),
        cost_estimate=cost(4 * cols * part * toks, 2 * (base.size + 2 * mine.size)),
        compiler_params=params(20),
        name="base_product",
    )(core, base, mine, other, low)


def low_kernel(rank, part, slots, *refs):
    count = len(refs) - 5
    blocks, (mine, other, old, new, ups) = refs[:count], refs[count:]
    w = jnp.concatenate([r[:, :part] for r in blocks], axis=0)
    at = 0
    for r in blocks:
        ups[at:at + r.shape[0], :] = r[:, part:]
        at += r.shape[0]
    for o, ref in enumerate((mine, other)):
        product = nt(w, token_rows(ref))
        ids = token_ids(ref)
        total = old[o]
        for a in range(w.shape[0] // rank):
            hit = ids == slots[a].astype(f32)
            total = total + jnp.where(hit, product[a * rank:(a + 1) * rank], 0.0)
        new[o] = total


def low_product(rank, part, slots, blocks, mine, other, old):
    rows = sum(b.shape[0] for b in blocks)
    toks = mine.shape[0]
    lanes = blocks[0].shape[1] - part
    return pl.pallas_call(
        functools.partial(low_kernel, rank, part),
        in_specs=[SMEM] + [VMEM] * (len(blocks) + 3),
        out_specs=[VMEM] * 2,
        out_shape=[jax.ShapeDtypeStruct(old.shape, f32), jax.ShapeDtypeStruct((rows, lanes), bf16)],
        cost_estimate=cost(4 * rows * part * toks, 2 * rows * part),
        compiler_params=params(20),
        name="low_product",
    )(slots, *blocks, mine, other, old)


def final_kernel(rank, wide, slots, got, u_mine, u_other, ids, out):
    rows = got.shape[2]
    cols = got.shape[1] - rank
    base = []
    low = jnp.zeros((rank, rows), f32)
    for c in range(2):
        total = jnp.zeros((cols, rows), f32)
        for x in range(4):
            total = total + got[2 * x + c, :cols, :].astype(f32)
            low = low + got[2 * x + c, cols:, :].astype(f32)
        base.append(total)
    base = jnp.concatenate(
        [base[c][t * wide:(t + 1) * wide] for t in range(cols // wide) for c in range(2)], axis=0
    )
    low = low.astype(bf16).astype(f32)
    names = ids[0:1, :].astype(f32)
    delta = None
    for o, u in enumerate((u_mine, u_other)):
        count = u.shape[0] // rank
        spread = jnp.concatenate(
            [jnp.where(names == slots[o * count + a].astype(f32), low, 0.0) for a in range(count)], axis=0
        )
        term = jnp.dot(spread.T.astype(bf16), u[...], preferred_element_type=f32)
        delta = term if delta is None else delta + term
    out[...] = (base.T + delta.astype(bf16).astype(f32)).astype(bf16)


def finish(rank, wide, slots, got, u_mine, u_other, ids):
    rows = got.shape[2]
    return pl.pallas_call(
        functools.partial(final_kernel, rank, wide),
        in_specs=[SMEM] + [VMEM] * 4,
        out_specs=VMEM,
        out_shape=jax.ShapeDtypeStruct((rows, 2 * (got.shape[1] - rank)), bf16),
        cost_estimate=cost(4 * u_mine.size * rows, 2 * got.size),
        compiler_params=params(20),
        name="finish",
    )(slots, got, u_mine, u_other, ids)


def on_device(tokens, base_key_weight, adapter_down_factors, adapter_up_factors, token_adapter_index, placement):
    rows, width = tokens.shape
    xl, xh, z, c = (lax.axis_index(a) for a in ("xl", "xh", "z", "c"))
    x = 2 * xh + xl
    part = width // 4
    table = placement.shape[0]
    rank = adapter_up_factors.shape[1]
    columns = jnp.arange(table, dtype=i32)
    core = c.astype(i32).reshape(1)

    down = adapter_down_factors[0].T
    up = adapter_up_factors[0]

    def factor_slice(at):
        d = lax.dynamic_slice(down, (0, at * part), (rank, part))
        return jnp.concatenate([d, up], axis=1)

    own = factor_slice(x)
    facing = lax.ppermute(
        factor_slice(3 - x), AXES, pairs_of(lambda xl, y, xh, z, c: (1 - xl, y, 1 - xh, z, c))
    )
    ring = pairs_of(lambda xl, y, xh, z, c: (xl, y, xh, z + 1 - 2 * c, c))
    a = jnp.concatenate([own, shift(own, "c", 1)], axis=0)
    b = jnp.concatenate([facing, shift(facing, "c", 1)], axis=0)
    held = [own, facing]
    for step in range(1, 5):
        a = lax.ppermute(a if step < 4 else a[:rank], AXES, ring)
        b = lax.ppermute(b if step < 4 else b[:rank], AXES, ring)
        held += [a, b]

    id_hot = (token_adapter_index == columns[None, :]).astype(i32)
    slot_ids = jnp.sum(id_hot * placement[None, :], axis=1)
    id_rows = jnp.broadcast_to(slot_ids.astype(bf16)[None, :], (8, rows))
    packed = pack(tokens, id_rows)
    mine = exchange(packed, XRING).reshape(4 * rows, part + LANES)
    other = shift(mine, "c", 1)

    panel = base_key_weight.T
    wide = panel.shape[0] // 2
    panel = lax.dynamic_slice(panel, (c * wide, 0), (wide, width))
    to_xl = [lax.dynamic_slice(panel, (0, (2 * xh + d) * part), (wide, part)) for d in range(2)]
    panels = jnp.concatenate([jnp.broadcast_to(p[None], (8, wide, part)) for p in to_xl], axis=0)
    base = exchange(panels, ("xl", "y")).reshape(16 * wide, part)

    def slot_list(cc):
        def at(side, off, core_at):
            return 16 * (xh if side == 0 else 1 - xh) + 2 * jnp.bitwise_and(z + off + 8, 7) + core_at

        out = [at(0, 0, cc), at(1, 0, cc)]
        for step in range(1, 4):
            off = step * (2 * cc - 1)
            for side in range(2):
                out += [at(side, off, cc), at(side, off, 1 - cc)]
        return jnp.stack(out + [at(0, 4, cc), at(1, 4, cc)]).astype(i32)

    slots_mine, slots_other = slot_list(c), slot_list(1 - c)
    low = jnp.zeros((2, rank, 4 * rows), f32)
    ups = []
    for k, (first, end) in enumerate(((0, 5), (5, 10))):
        low, u = low_product(rank, part, slots_mine[8 * k:8 * k + 8], held[first:end], mine, other, low)
        ups.append(u)
    u_mine = join(ups)
    u_other = shift(u_mine, "c", 1)

    out = base_product(core, base, mine, other, low)
    got = exchange(out, ("xh", "xl", "c"))
    slots = jnp.concatenate([slots_mine, slots_other])
    return finish(rank, wide, slots, got, u_mine, u_other, id_rows)


def solution(mesh):
    fine = Mesh(mesh.devices.reshape(SIZES), AXES)
    whole = ("xl", "y", "xh", "z", "c")
    adapter = ("xh", "z", "c")

    return jax.shard_map(
        on_device,
        mesh=fine,
        in_specs=(
            P(whole, None),
            P(None, ("xl", "y")),
            P(adapter, None, None),
            P(adapter, None, None),
            P(whole, None),
            P(),
        ),
        out_specs=P(whole, None),
        check_vma=False,
    )
```
